32 devices in a mesh: dp: 4 (over y, x), ctx: 4 (over z), tp: 2 (over core).
Axes of the slice: x: 2, y: 2, z: 4, core: 2. Of those that a mesh axis runs over, the one named last changes fastest.
Arguments:
- tokens: float32 [4, 1024, 768], P('dp', 'ctx'), may hold values from -6 to 6
- cotangent: float32 [4, 1024, 768], P('dp', 'ctx'), may hold values from -6 to 6
- mat_in: float32 [768, 2, 1548], P('dp', 'tp'), may hold values from -0.21875 to 0.21875
- mat_bc: float32 [768, 256], P('dp'), may hold values from -0.21875 to 0.21875
- mat_out: float32 [1536, 768], P('tp', 'dp'), may hold values from -0.15625 to 0.15625
- vec_split: float32 [2, 4644], P('tp'), may hold values from -7.61 to 1.5, as said below
- vec_rep: float32 [2048], replicated, may hold values from -1.5 to 1.5, as said below
- mom_in: float32 [2, 768, 2, 1548], P(None, 'dp', 'tp'), may hold values from -40 to 40, as said below
- mom_bc: float32 [2, 768, 256], P(None, 'dp'), may hold values from -40 to 40, as said below
- mom_out: float32 [2, 1536, 768], P(None, 'tp', 'dp'), may hold values from -40 to 40, as said below
- mom_split: float32 [2, 2, 4644], P(None, 'tp'), may hold values from -40 to 40, as said below
- mom_rep: float32 [2, 2048], replicated, may hold values from -40 to 40, as said below
Outputs:
- block_out: float32 [4, 1024, 768], P('dp', 'ctx')
- input_grad: float32 [4, 1024, 768], P('dp', 'ctx')
- new_mat_in: float32 [768, 2, 1548], P('dp', 'tp')
- new_mat_bc: float32 [768, 256], P('dp')
- new_mat_out: float32 [1536, 768], P('tp', 'dp')
- new_vec_split: float32 [2, 4644], P('tp')
- new_vec_rep: float32 [2048], replicated
- new_mom_in: float32 [2, 768, 2, 1548], P(None, 'dp', 'tp')
- new_mom_bc: float32 [2, 768, 256], P(None, 'dp')
- new_mom_out: float32 [2, 1536, 768], P(None, 'tp', 'dp')
- new_mom_split: float32 [2, 2, 4644], P(None, 'tp')
- new_mom_rep: float32 [2, 2048], replicated
The draws below stay inside these ranges and needn't reach their ends.
Inputs may be any that keep to these rules, and one draw needn't show every extreme that they name: `vec_split`: laid out as the steps say; gate gains between 0.6 and 1.4, A_log between log(0.0005) and log(0.1), step biases between -4 and -1. `vec_rep`: laid out as the steps say; the gain between 0.6 and 1.4. `mom_in`: index 1 of the first dimension (second moments) lies between 1 and 30. `mom_bc`: index 1 of the first dimension (second moments) lies between 1 and 30. `mom_out`: index 1 of the first dimension (second moments) lies between 1 and 30. `mom_split`: index 1 of the first dimension (second moments) lies between 1 and 30. `mom_rep`: index 1 of the first dimension (second moments) lies between 1 and 30.
All inputs are finite; a program needn't handle non-finite values.
Results may differ from the reference program's by a relative error of at most 0.0014.
The reference program's roundings to bfloat16 on the way count: a program that leaves them out, or rounds other values in their place, can miss the bound.
Values may be sent and summed in bfloat16 or wider, within the bound.
A program may use at most 128 MiB of HBM per device.

```python
import math
import jax
import jax.numpy as jnp
from jax import lax

D = 768
H = 24
P_SIZE = 64
N = 128
KC = 4
SPAN = 256
E = 1536
EL = 768
HL = 12
CT = 1548
VS = 4644
VR = 2048
LEN = 1024
SEQS = 4


def draw_moment_pair(key, shape):
    first_key = jax.random.fold_in(key, 11)
    second_key = jax.random.fold_in(key, 12)
    first_mom = jnp.clip(10.0 * jax.random.normal(first_key, shape, jnp.float32), -40.0, 40.0)
    second_mom = jnp.exp(jax.random.uniform(second_key, shape, jnp.float32, 0.0, math.log(30.0)))
    return jnp.stack([first_mom, second_mom])


def draw_vec_split(key, part):
    groups = E // EL
    key_list = [jax.random.fold_in(key, 21 + offset) for offset in range(6)]
    conv_w = jnp.clip(0.5 * jax.random.normal(key_list[0], (groups, KC * EL), jnp.float32), -1.5, 1.5)
    conv_b = jax.random.uniform(key_list[1], (groups, EL), jnp.float32, -0.5, 0.5)
    gate_gain = jax.random.uniform(key_list[2], (groups, EL), jnp.float32, 0.6, 1.4)
    step_bias = jax.random.uniform(key_list[3], (groups, HL), jnp.float32, -4.0, -1.0)
    rate_log = jax.random.uniform(key_list[4], (groups, HL), jnp.float32, math.log(0.0005), math.log(0.1))
    skip_gain = jax.random.uniform(key_list[5], (groups, HL), jnp.float32, 0.5, 1.5)
    return jnp.concatenate([conv_w, conv_b, gate_gain, step_bias, rate_log, skip_gain], axis=1)


def draw_vec_rep(key, part):
    key_list = [jax.random.fold_in(key, 31 + offset) for offset in range(3)]
    norm_gain = jax.random.uniform(key_list[0], (D,), jnp.float32, 0.6, 1.4)
    conv_w = jnp.clip(0.5 * jax.random.normal(key_list[1], (KC * 2 * N,), jnp.float32), -1.5, 1.5)
    conv_b = jax.random.uniform(key_list[2], (2 * N,), jnp.float32, -0.5, 0.5)
    return jnp.concatenate([norm_gain, conv_w, conv_b])


def draw_mom_in(key, part):
    return draw_moment_pair(key, (D, E // EL, CT))


def draw_mom_bc(key, part):
    return draw_moment_pair(key, (D, 2 * N))


def draw_mom_out(key, part):
    return draw_moment_pair(key, (E, D))


def draw_mom_split(key, part):
    return draw_moment_pair(key, (E // EL, VS))


def draw_mom_rep(key, part):
    return draw_moment_pair(key, (VR,))


def level_of(stream_key, dims, cuts, smallest, top_value):
    factor_of = 1.0
    for axis_at, shards_of in cuts:
        steps = jax.random.uniform(jax.random.fold_in(jax.random.fold_in(stream_key, 6), axis_at), (shards_of,), jnp.float32, smallest / len(cuts), top_value / len(cuts))
        factor_of = factor_of * jnp.repeat(jnp.exp(steps), dims[axis_at] // shards_of).reshape((-1,) + (1,) * (len(dims) - 1 - axis_at))
    return factor_of


def bell_draw(stream_key, extent, deviation, reach, cuts=(), kind=jnp.bfloat16):
    values = jax.random.normal(stream_key, extent, jnp.float32) * deviation
    if len(cuts) > 0:
        values = level_of(stream_key, extent, cuts, -0.22, 0.18) * values
    return jnp.clip(values, min=-reach, max=reach).astype(kind)


def setup_inputs(seed: int = 0) -> dict:
    streams_of = jax.random.split(jax.random.key(seed), 13)
    return {
        "tokens": bell_draw(streams_of[0], (SEQS, LEN, D), 1.0, 6.0, ((0, 4), (1, 4)), jnp.float32),
        "cotangent": bell_draw(streams_of[1], (SEQS, LEN, D), 1.0, 6.0, ((0, 4), (1, 4)), jnp.float32),
        "mat_in": bell_draw(streams_of[2], (D, E // EL, CT), D ** -0.5, 0.21875, ((0, 4), (1, 2)), jnp.float32),
        "mat_bc": bell_draw(streams_of[3], (D, 2 * N), D ** -0.5, 0.21875, ((0, 4),), jnp.float32),
        "mat_out": bell_draw(streams_of[4], (E, D), E ** -0.5, 0.15625, ((0, 2), (1, 4)), jnp.float32),
        "vec_split": draw_vec_split(jax.random.fold_in(streams_of[12], 71), 0),
        "vec_rep": draw_vec_rep(jax.random.fold_in(streams_of[12], 71), 0),
        "mom_in": draw_mom_in(jax.random.fold_in(streams_of[12], 71), 0),
        "mom_bc": draw_mom_bc(jax.random.fold_in(streams_of[12], 71), 0),
        "mom_out": draw_mom_out(jax.random.fold_in(streams_of[12], 71), 0),
        "mom_split": draw_mom_split(jax.random.fold_in(streams_of[12], 71), 0),
        "mom_rep": draw_mom_rep(jax.random.fold_in(streams_of[12], 71), 0),
    }


norm_eps = 1e-05
adam_beta1 = 0.9
adam_beta2 = 0.999
adam_eps = 1e-08
learn_rate = 0.01
decay_rate = 0.1
adam_count = 2.0
top_precision = lax.Precision.HIGHEST

def conv_apply(padded, weights, biases):
    tap_count = weights.shape[0]
    length = padded.shape[0] - tap_count + 1
    summed = jnp.zeros((length, padded.shape[1]), jnp.float32) + biases[None, :]
    for offset in range(tap_count):
        summed = summed + weights[offset][None, :] * padded[offset:offset + length]
    return jax.nn.silu(summed)

def span_terms(x_heads, b_state, c_state, dt_heads, neg_rates, state_in):
    length = x_heads.shape[0]
    cumulated = jnp.cumsum(dt_heads * neg_rates[None, :], axis=0)
    cum_heads = cumulated.T
    row_pos = lax.broadcasted_iota(jnp.int32, (length, length), 0)
    col_pos = lax.broadcasted_iota(jnp.int32, (length, length), 1)
    causal = (col_pos <= row_pos)[None, :, :]
    differ = cum_heads[:, :, None] - cum_heads[:, None, :]
    decays = jnp.where(causal, jnp.exp(jnp.where(causal, differ, 0.0)), 0.0)
    scores = jnp.dot(c_state, b_state.T, precision=top_precision)
    mixing = scores[None, :, :] * decays * dt_heads.T[:, None, :]
    inside = jnp.einsum('hts,shp->thp', mixing, x_heads, precision=top_precision)
    carried = jnp.exp(cumulated)[:, :, None] * jnp.einsum('tn,hpn->thp', c_state, state_in, precision=top_precision)
    ending = cumulated[-1]
    weights_tail = jnp.exp(ending[None, :] - cumulated) * dt_heads
    state_out = jnp.exp(ending)[:, None, None] * state_in + jnp.einsum('sh,shp,sn->hpn', weights_tail, x_heads, b_state, precision=top_precision)
    return (inside + carried, state_out)

def ssd_sequence(x_cols, b_state, c_state, dt_raw, step_bias, rate_log, skip_gain):
    length = x_cols.shape[0]
    blocks = length // SPAN
    steps_dt = jax.nn.softplus(dt_raw + step_bias[None, :])
    neg_rates = -jnp.exp(rate_log)

    def advance(state_now, pieces):
        x_part, b_part, c_part, dt_part = pieces
        result, state_next = span_terms(x_part, b_part, c_part, dt_part, neg_rates, state_now)
        return (state_next, result)
    start_state = jnp.zeros((H, P_SIZE, N), jnp.float32)
    final_state, outputs = lax.scan(advance, start_state, (x_cols.reshape(blocks, SPAN, H, P_SIZE), b_state.reshape(blocks, SPAN, N), c_state.reshape(blocks, SPAN, N), steps_dt.reshape(blocks, SPAN, H)))
    mixed = outputs.reshape(length, H, P_SIZE) + skip_gain[None, :, None] * x_cols.reshape(length, H, P_SIZE)
    return mixed.reshape(length, E)

def adam_step(weights, moments, grads):
    first_mom = adam_beta1 * moments[0] + (1.0 - adam_beta1) * grads
    second_mom = adam_beta2 * moments[1] + (1.0 - adam_beta2) * grads * grads
    first_hat = first_mom / (1.0 - adam_beta1 ** adam_count)
    second_hat = second_mom / (1.0 - adam_beta2 ** adam_count)
    updated = weights - learn_rate * (first_hat / (jnp.sqrt(second_hat) + adam_eps) + decay_rate * weights)
    return (updated, jnp.stack([first_mom, second_mom]))

def reference(tokens, cotangent, mat_in, mat_bc, mat_out, vec_split, vec_rep, mom_in, mom_bc, mom_out, mom_split, mom_rep):
    groups = E // EL
    weight_z = mat_in[:, :, :EL].reshape(D, E)
    weight_x = mat_in[:, :, EL:2 * EL].reshape(D, E)
    weight_dt = mat_in[:, :, 2 * EL:].reshape(D, H)
    bf_split = jnp.concatenate([weight_z, weight_x, weight_dt], axis=1).astype(jnp.bfloat16)
    bf_bc = mat_bc.astype(jnp.bfloat16)
    bf_out = mat_out.astype(jnp.bfloat16)
    conv_x_w = vec_split[:, :KC * EL].reshape(groups, KC, EL).transpose(1, 0, 2).reshape(KC, E)
    conv_end = KC * EL
    conv_x_b = vec_split[:, conv_end:conv_end + EL].reshape(E)
    gate_gain = vec_split[:, conv_end + EL:conv_end + 2 * EL].reshape(E)
    head_base = conv_end + 2 * EL
    step_bias = vec_split[:, head_base:head_base + HL].reshape(H)
    rate_log = vec_split[:, head_base + HL:head_base + 2 * HL].reshape(H)
    skip_gain = vec_split[:, head_base + 2 * HL:].reshape(H)
    norm_gain = vec_rep[:D]
    conv_bc_w = vec_rep[D:D + KC * 2 * N].reshape(KC, 2 * N)
    conv_bc_b = vec_rep[D + KC * 2 * N:]
    conv_all_w = jnp.concatenate([conv_x_w, conv_bc_w], axis=1)
    conv_all_b = jnp.concatenate([conv_x_b, conv_bc_b])

    def one_sequence(totals, pair):
        seq_tokens, seq_cotan = pair
        inv_rms = lax.rsqrt(lax.optimization_barrier(jnp.mean(seq_tokens * seq_tokens, axis=1, keepdims=True)) + norm_eps)
        normed = (seq_tokens * inv_rms * norm_gain[None, :]).astype(jnp.bfloat16)
        proj_split = jnp.dot(normed, bf_split, preferred_element_type=jnp.float32)
        proj_bc = jnp.dot(normed, bf_bc, preferred_element_type=jnp.float32)
        proj_z = proj_split[:, :E]
        proj_dt = proj_split[:, 2 * E:]
        pre_conv = jnp.concatenate([proj_split[:, E:2 * E], proj_bc], axis=1)
        padded = jnp.pad(pre_conv, ((KC - 1, 0), (0, 0)))
        activated, conv_back = jax.vjp(conv_apply, padded, conv_all_w, conv_all_b)
        x_cols = activated[:, :E]
        b_state = activated[:, E:E + N]
        c_state = activated[:, E + N:]
        mixed, ssd_back = jax.vjp(ssd_sequence, x_cols, b_state, c_state, proj_dt, step_bias, rate_log, skip_gain)
        gate_act = jax.nn.silu(proj_z)
        gated = mixed * gate_act
        gate_rms = lax.rsqrt(lax.optimization_barrier(jnp.mean(gated * gated, axis=1, keepdims=True)) + norm_eps)
        outnorm = (gated * gate_rms * gate_gain[None, :]).astype(jnp.bfloat16)
        block_out = seq_tokens + jnp.dot(outnorm, bf_out, preferred_element_type=jnp.float32)
        cotan_b = seq_cotan.astype(jnp.bfloat16)
        grad_norm_out = jnp.dot(cotan_b, bf_out.T, preferred_element_type=jnp.float32)
        grad_w_out = jnp.dot(outnorm.T, cotan_b, preferred_element_type=jnp.float32)
        grad_gate_gain = lax.optimization_barrier(jnp.sum(grad_norm_out * gated * gate_rms, axis=0))
        inner_sum = lax.optimization_barrier(jnp.mean(grad_norm_out * gate_gain[None, :] * gated, axis=1, keepdims=True))
        grad_gated = gate_rms * gate_gain[None, :] * grad_norm_out - gated * gate_rms ** 3 * inner_sum
        grad_mixed = grad_gated * gate_act
        sigmoid_z = jax.nn.sigmoid(proj_z)
        grad_z = grad_gated * mixed * sigmoid_z * (1.0 + proj_z * (1.0 - sigmoid_z))
        grad_x, grad_b, grad_c, grad_dt, grad_step_bias, grad_rate_log, grad_skip = ssd_back(grad_mixed)
        grad_pad, grad_conv_w, grad_conv_b = conv_back(jnp.concatenate([grad_x, grad_b, grad_c], axis=1))
        grad_pre = grad_pad[KC - 1:]
        grad_split = jnp.concatenate([grad_z, grad_pre[:, :E], grad_dt], axis=1).astype(jnp.bfloat16)
        grad_bc = grad_pre[:, E:].astype(jnp.bfloat16)
        grad_hidden = jnp.dot(grad_split, bf_split.T, preferred_element_type=jnp.float32) + jnp.dot(grad_bc, bf_bc.T, preferred_element_type=jnp.float32)
        grad_norm_gain = lax.optimization_barrier(jnp.sum(grad_hidden * seq_tokens * inv_rms, axis=0))
        inner_in = lax.optimization_barrier(jnp.mean(grad_hidden * norm_gain[None, :] * seq_tokens, axis=1, keepdims=True))
        grad_tokens = seq_cotan + inv_rms * norm_gain[None, :] * grad_hidden - seq_tokens * inv_rms ** 3 * inner_in
        grad_w_split = jnp.dot(normed.T, grad_split, preferred_element_type=jnp.float32)
        grad_w_bc = jnp.dot(normed.T, grad_bc, preferred_element_type=jnp.float32)
        fresh = (grad_w_split, grad_w_bc, grad_w_out, grad_conv_w, grad_conv_b, grad_gate_gain, grad_step_bias, grad_rate_log, grad_skip, grad_norm_gain)
        new_totals = jax.tree.map(lambda current, addend: current + addend, totals, fresh)
        return (new_totals, (block_out, grad_tokens))
    start_totals = (jnp.zeros((D, 2 * E + H), jnp.float32), jnp.zeros((D, 2 * N), jnp.float32), jnp.zeros((E, D), jnp.float32), jnp.zeros((KC, E + 2 * N), jnp.float32), jnp.zeros((E + 2 * N,), jnp.float32), jnp.zeros((E,), jnp.float32), jnp.zeros((H,), jnp.float32), jnp.zeros((H,), jnp.float32), jnp.zeros((H,), jnp.float32), jnp.zeros((D,), jnp.float32))
    totals, outputs = lax.scan(one_sequence, start_totals, (tokens, cotangent))
    block_all, grad_all = outputs
    grad_w_split, grad_w_bc, grad_w_out, grad_conv_w, grad_conv_b, grad_gate_gain, grad_step_bias, grad_rate_log, grad_skip, grad_norm_gain = totals
    grad_mat_in = jnp.concatenate([grad_w_split[:, :E].reshape(D, groups, EL), grad_w_split[:, E:2 * E].reshape(D, groups, EL), grad_w_split[:, 2 * E:].reshape(D, groups, HL)], axis=2)
    grad_vec_split = jnp.concatenate([grad_conv_w[:, :E].reshape(KC, groups, EL).transpose(1, 0, 2).reshape(groups, KC * EL), grad_conv_b[:E].reshape(groups, EL), grad_gate_gain.reshape(groups, EL), grad_step_bias.reshape(groups, HL), grad_rate_log.reshape(groups, HL), grad_skip.reshape(groups, HL)], axis=1)
    grad_vec_rep = jnp.concatenate([grad_norm_gain, grad_conv_w[:, E:].reshape(KC * 2 * N), grad_conv_b[E:]])
    new_in, new_mom_in = adam_step(mat_in, mom_in, grad_mat_in)
    new_bc, new_mom_bc = adam_step(mat_bc, mom_bc, grad_w_bc)
    new_out, new_mom_out = adam_step(mat_out, mom_out, grad_w_out)
    new_split, new_mom_split = adam_step(vec_split, mom_split, grad_vec_split)
    new_rep, new_mom_rep = adam_step(vec_rep, mom_rep, grad_vec_rep)
    return (block_all, grad_all, new_in, new_bc, new_out, new_split, new_rep, new_mom_in, new_mom_bc, new_mom_out, new_mom_split, new_mom_rep)
```

```python
import functools

import jax
import jax.numpy as jnp
from jax import lax
from jax.experimental import pallas as pl
from jax.experimental.pallas import tpu as pltpu
from jax.sharding import PartitionSpec as P

D = 768
KC = 4
E = 1536


norm_eps = 1e-05
adam_beta1 = 0.9
adam_beta2 = 0.999
adam_eps = 1e-08
learn_rate = 0.01
decay_rate = 0.1
adam_count = 2.0
top_precision = lax.Precision.HIGHEST


def shifted(block, axis, distance):
    devices = range(lax.axis_size(axis))
    route = [(i - distance, i) for i in devices if i - distance in devices]
    return lax.ppermute(block, axis, route)


def entering(value, axis, join, neutral, backward):
    count, mine = (lax.axis_size(axis), lax.axis_index(axis))
    pieces = jax.tree.map(lambda part: lax.all_gather(part, axis), value)
    if backward:
        pieces = jax.tree.map(lambda part: part[::-1], pieces)
        mine = count - 1 - mine
    subtotal = jax.tree.map(
        lambda part, zero: jnp.full_like(part, 0) + jnp.asarray(zero, part.dtype), value, neutral
    )

    def turn(position, subtotal):
        longer = join(subtotal, jax.tree.map(lambda part: part[position], pieces))
        return jax.tree.map(lambda new, old: jnp.where(position < mine, new, old), longer, subtotal)

    return lax.fori_loop(0, count - 1, turn, subtotal)


def conv_apply(padded, weights, biases):
    tap_count = weights.shape[0]
    length = padded.shape[0] - tap_count + 1
    summed = jnp.zeros((length, padded.shape[1]), jnp.float32) + biases[None, :]
    for offset in range(tap_count):
        summed = summed + weights[offset][None, :] * padded[offset : offset + length]
    return jax.nn.silu(summed)


def span_terms(x_heads, b_state, c_state, dt_heads, neg_rates, state_in):
    length = x_heads.shape[0]
    cumulated = jnp.cumsum(dt_heads * neg_rates[None, :], axis=0)
    cum_heads = cumulated.T
    row_pos = lax.broadcasted_iota(jnp.int32, (length, length), 0)
    col_pos = lax.broadcasted_iota(jnp.int32, (length, length), 1)
    causal = (col_pos <= row_pos)[None, :, :]
    differ = cum_heads[:, :, None] - cum_heads[:, None, :]
    decays = jnp.where(causal, jnp.exp(jnp.where(causal, differ, 0.0)), 0.0)
    scores = jnp.dot(c_state, b_state.T, precision=top_precision)
    mixing = scores[None, :, :] * decays * dt_heads.T[:, None, :]
    inside = jnp.einsum("hts,shp->thp", mixing, x_heads, precision=top_precision)
    carried = jnp.exp(cumulated)[:, :, None] * jnp.einsum(
        "tn,hpn->thp", c_state, state_in, precision=top_precision
    )
    ending = cumulated[-1]
    weights_tail = jnp.exp(ending[None, :] - cumulated) * dt_heads
    state_out = jnp.exp(ending)[:, None, None] * state_in + jnp.einsum(
        "sh,shp,sn->hpn", weights_tail, x_heads, b_state, precision=top_precision
    )
    return (inside + carried, state_out)


def local_mixer(x_cols, b_state, c_state, dt_raw, step_bias, rate_log, skip_gain):
    rows_here = x_cols.shape[0]
    head_count = dt_raw.shape[1]
    head_width = x_cols.shape[1] // head_count
    steps_dt = jax.nn.softplus(dt_raw + step_bias[None, :])
    neg_rates = -jnp.exp(rate_log)
    x_heads = x_cols.reshape(rows_here, head_count, head_width)
    state_now = jnp.zeros((head_count, head_width, b_state.shape[1]), jnp.float32)
    part_out, state_now = span_terms(x_heads, b_state, c_state, steps_dt, neg_rates, state_now)
    pieces = [part_out]
    cumulated = jnp.cumsum(steps_dt * neg_rates[None, :], axis=0)
    mixed = jnp.concatenate(pieces, axis=0) + skip_gain[None, :, None] * x_heads
    return (mixed, state_now, jnp.exp(cumulated[-1]), cumulated)


def carried_in(cumulated, c_state, start_state):
    return jnp.exp(cumulated)[:, :, None] * jnp.einsum(
        "tn,hpn->thp", c_state, start_state, precision=top_precision
    )


def chain_link(earlier, latter):
    return (earlier[0] * latter[0], earlier[1] * latter[0][:, None, None] + latter[1])


lane = 128
chunk_lanes = 4
mesh_ids = pl.DeviceIdType.MESH


def greet(peers):
    barrier = pltpu.get_barrier_semaphore()
    for peer in peers:
        pl.semaphore_signal(barrier, inc=1, device_id=peer, device_id_type=mesh_ids)
    pl.semaphore_wait(barrier, len(peers))


def others(axis, count):
    mine = lax.axis_index(axis)
    return [lax.rem(mine + step, count) for step in range(1, count)]


def send(src, dst, sent, got, axis, peer):
    copy = pltpu.make_async_remote_copy(
        src_ref=src,
        dst_ref=dst,
        send_sem=sent,
        recv_sem=got,
        device_id={axis: peer},
        device_id_type=mesh_ids,
    )
    copy.start()
    return copy


def column_chunks(width):
    step = chunk_lanes * lane
    return [(at, min(step, width - at)) for at in range(0, width, step)]


def reduce_body(
    dp_count, ctx_count, a_ref, b_ref, s_ref, out_a, out_b, out_pair, out_s,
    slot_a, slot_b, red_a, red_b, zslot_a, zslot_b, all_a, all_b, pair_slot,
    s_slot, s_red, s_zslot,
    sent1, got1, sent2, got2, sent3, got3, s_sent, s_got, pair_sent, pair_got,
):
    me = lax.axis_index("dp")
    here = lax.axis_index("ctx")
    dp_peers = others("dp", dp_count)
    ctx_peers = others("ctx", ctx_count)
    partner = 1 - lax.axis_index("tp")
    greet(
        [{"dp": peer} for peer in dp_peers]
        + [{"ctx": peer} for peer in ctx_peers]
        + [{"tp": partner}]
    )
    wide = a_ref.shape[3]
    half = wide - lane
    chunks = [(0, half, lane)]
    chunks += [(0, at, size) for at, size in column_chunks(half)]
    chunks += [(1, at, size) for at, size in column_chunks(b_ref.shape[3])]
    sources = (a_ref, b_ref)
    slots, reds, zslots, alls = (slot_a, slot_b), (red_a, red_b), (zslot_a, zslot_b), (all_a, all_b)
    waits = []

    s_copies = []
    for step, peer in enumerate(dp_peers):
        s_copies.append(send(s_ref, s_slot.at[me], s_sent.at[0, step], s_got.at[0, step], "dp", peer))
    first = []
    for number, (which, at, size) in enumerate(chunks):
        cols = pl.ds(at, size)
        first.append([
            send(
                sources[which].at[peer, :, :, cols],
                slots[which].at[step, :, :, cols],
                sent1.at[number, step],
                got1.at[number, step],
                "dp",
                peer,
            )
            for step, peer in enumerate(dp_peers)
        ])
    s_slot[me] = s_ref[...]
    for copy in s_copies:
        copy.wait_recv()
    total = s_slot[0]
    for step in range(1, dp_count):
        total = total + s_slot[step]
    s_red[...] = total
    s_zslot[here] = total
    z_copies = []
    for step, peer in enumerate(ctx_peers):
        z_copies.append(
            send(s_red, s_zslot.at[here], s_sent.at[1, step], s_got.at[1, step], "ctx", peer)
        )
    waits += s_copies + z_copies

    second = []
    third = []

    def scatter(number):
        which, at, size = chunks[number]
        cols = pl.ds(at, size)
        for copy in first[number]:
            copy.wait_recv()
        total = sources[which][me, :, :, cols]
        for step in range(dp_count - 1):
            total = total + slots[which][step, :, :, cols]
        reds[which][:, :, cols] = total
        second.append([
            send(
                reds[which].at[peer, :, cols],
                zslots[which].at[step, :, cols],
                sent2.at[number, step],
                got2.at[number, step],
                "ctx",
                peer,
            )
            for step, peer in enumerate(ctx_peers)
        ])

    def gather(number):
        which, at, size = chunks[number]
        cols = pl.ds(at, size)
        for copy in second[number]:
            copy.wait_recv()
        total = reds[which][here, :, cols]
        for step in range(ctx_count - 1):
            total = total + zslots[which][step, :, cols]
        alls[which][here, :, cols] = total
        third.append([
            send(
                alls[which].at[here, :, cols],
                alls[which].at[here, :, cols],
                sent3.at[number, step],
                got3.at[number, step],
                "ctx",
                peer,
            )
            for step, peer in enumerate(ctx_peers)
        ])

    def exchange():
        for copy in third[0]:
            copy.wait_recv()
        return send(
            all_a.at[:, :, pl.ds(half, lane)], pair_slot, pair_sent, pair_got, "tp", partner
        )

    pair = None
    for number in range(len(chunks) + 1):
        if number < len(chunks):
            scatter(number)
        if number >= 1:
            gather(number - 1)
        if number == 2:
            pair = exchange()
    for copy in z_copies:
        copy.wait_recv()
    total = s_zslot[0]
    for step in range(1, ctx_count):
        total = total + s_zslot[step]
    out_s[...] = total
    outs = (out_a, out_b)
    for number, (which, at, size) in enumerate(chunks):
        cols = pl.ds(at, size)
        if number > 0:
            for copy in third[number]:
                copy.wait_recv()
        outs[which][:, :, cols] = alls[which][:, :, cols]
    pair.wait_recv()
    out_pair[...] = pair_slot[...]
    pair.wait_send()
    for group in first + second + third + [waits]:
        for copy in group:
            copy.wait_send()


def reduce_grads(grad_a, grad_b, small):
    dp_count, ctx_count = lax.axis_size("dp"), lax.axis_size("ctx")
    rows = grad_a.shape[0] // (dp_count * ctx_count)
    wide_a, wide_b = grad_a.shape[1], grad_b.shape[1]
    count = 1 + len(column_chunks(wide_a - lane)) + len(column_chunks(wide_b))
    f32 = jnp.float32
    vmem = pl.BlockSpec(memory_space=pltpu.VMEM)
    semaphores = [
        pltpu.SemaphoreType.DMA((count, dp_count - 1)),
        pltpu.SemaphoreType.DMA((count, dp_count - 1)),
        pltpu.SemaphoreType.DMA((count, ctx_count - 1)),
        pltpu.SemaphoreType.DMA((count, ctx_count - 1)),
        pltpu.SemaphoreType.DMA((count, ctx_count - 1)),
        pltpu.SemaphoreType.DMA((count, ctx_count - 1)),
        pltpu.SemaphoreType.DMA((2, max(dp_count, ctx_count))),
        pltpu.SemaphoreType.DMA((2, max(dp_count, ctx_count))),
        pltpu.SemaphoreType.DMA,
        pltpu.SemaphoreType.DMA,
    ]
    own_a, own_b = (ctx_count, rows, wide_a), (ctx_count, rows, wide_b)
    out_a, out_b, out_pair, out_s = pl.pallas_call(
        functools.partial(reduce_body, dp_count, ctx_count),
        out_shape=(
            jax.ShapeDtypeStruct(own_a, f32),
            jax.ShapeDtypeStruct(own_b, f32),
            jax.ShapeDtypeStruct((ctx_count, rows, lane), f32),
            jax.ShapeDtypeStruct(small.shape, f32),
        ),
        in_specs=[vmem] * 3,
        out_specs=(vmem,) * 4,
        scratch_shapes=[
            pltpu.VMEM((dp_count - 1,) + own_a, f32),
            pltpu.VMEM((dp_count - 1,) + own_b, f32),
            pltpu.VMEM(own_a, f32),
            pltpu.VMEM(own_b, f32),
            pltpu.VMEM((ctx_count - 1, rows, wide_a), f32),
            pltpu.VMEM((ctx_count - 1, rows, wide_b), f32),
            pltpu.VMEM(own_a, f32),
            pltpu.VMEM(own_b, f32),
            pltpu.VMEM((ctx_count, rows, lane), f32),
            pltpu.VMEM((dp_count,) + small.shape, f32),
            pltpu.VMEM(small.shape, f32),
            pltpu.VMEM((ctx_count,) + small.shape, f32),
        ]
        + semaphores,
        compiler_params=pltpu.CompilerParams(collective_id=0, has_side_effects=True),
        name="reduce_grads",
    )(
        grad_a.reshape((dp_count,) + own_a),
        grad_b.reshape((dp_count,) + own_b),
        small,
    )
    flat = lambda part: part.reshape(ctx_count * rows, part.shape[-1])
    return flat(out_a), flat(out_b), flat(out_pair), out_s


def adam_step(weights, moments, grads):
    first_mom = adam_beta1 * moments[0] + (1.0 - adam_beta1) * grads
    second_mom = adam_beta2 * moments[1] + (1.0 - adam_beta2) * grads * grads
    first_hat = first_mom / (1.0 - adam_beta1**adam_count)
    second_hat = second_mom / (1.0 - adam_beta2**adam_count)
    updated = weights - learn_rate * (
        first_hat / (jnp.sqrt(second_hat) + adam_eps) + decay_rate * weights
    )
    return (updated, jnp.stack([first_mom, second_mom]))


def shards(
    tokens,
    cotangent,
    mat_in,
    mat_bc,
    mat_out,
    vec_split,
    vec_rep,
    mom_in,
    mom_bc,
    mom_out,
    mom_split,
    mom_rep,
):
    full_in, full_bc, full_out = (
        lax.all_gather(mat_in.astype(jnp.bfloat16), "dp", axis=0, tiled=True),
        lax.all_gather(mat_bc.astype(jnp.bfloat16), "dp", axis=0, tiled=True),
        lax.all_gather(mat_out.astype(jnp.bfloat16), "dp", axis=1, tiled=True),
    )
    w_split = full_in[:, 0, :]
    local_inner = full_out.shape[0]
    local_heads = w_split.shape[1] - 2 * local_inner
    state_size = full_bc.shape[1] // 2
    taps_less = KC - 1
    seq_tokens = tokens[0]
    seq_cotan = cotangent[0]
    rows_here = seq_tokens.shape[0]
    split_row = vec_split[0]
    conv_x_w = split_row[: KC * local_inner].reshape(KC, local_inner)
    conv_end = KC * local_inner
    conv_x_b = split_row[conv_end : conv_end + local_inner]
    gate_gain = split_row[conv_end + local_inner : conv_end + 2 * local_inner]
    head_base = conv_end + 2 * local_inner
    step_bias = split_row[head_base : head_base + local_heads]
    rate_log = split_row[head_base + local_heads : head_base + 2 * local_heads]
    skip_gain = split_row[head_base + 2 * local_heads :]
    norm_gain = vec_rep[:D]
    conv_bc_w = vec_rep[D : D + KC * 2 * state_size].reshape(KC, 2 * state_size)
    conv_bc_b = vec_rep[D + KC * 2 * state_size :]
    conv_all_w = jnp.concatenate([conv_x_w, conv_bc_w], axis=1)
    conv_all_b = jnp.concatenate([conv_x_b, conv_bc_b])
    inv_rms = lax.rsqrt(jnp.mean(seq_tokens * seq_tokens, axis=1, keepdims=True) + norm_eps)
    normed = (seq_tokens * inv_rms * norm_gain[None, :]).astype(jnp.bfloat16)
    proj_split = jnp.dot(normed, w_split, preferred_element_type=jnp.float32)
    proj_bc = jnp.dot(normed, full_bc, preferred_element_type=jnp.float32)
    proj_z = proj_split[:, :local_inner]
    proj_dt = proj_split[:, 2 * local_inner :]
    pre_conv = jnp.concatenate([proj_split[:, local_inner : 2 * local_inner], proj_bc], axis=1)
    rim_rows = shifted(pre_conv[rows_here - taps_less :], "ctx", 1)
    padded = jnp.concatenate([rim_rows, pre_conv], axis=0)
    activated, conv_back = jax.vjp(conv_apply, padded, conv_all_w, conv_all_b)
    x_cols = activated[:, :local_inner]
    b_state = activated[:, local_inner : local_inner + state_size]
    c_state = activated[:, local_inner + state_size :]
    mixer_out, mixer_back = jax.vjp(
        local_mixer, x_cols, b_state, c_state, proj_dt, step_bias, rate_log, skip_gain
    )
    zero_mixed, local_state, decay_dev, cumulated = mixer_out
    chain_ones = jnp.ones_like(decay_dev)
    chain_zero = jnp.zeros_like(local_state)
    prior_decay, start_state = entering(
        (decay_dev, local_state), "ctx", chain_link, (chain_ones, chain_zero), False
    )
    carried, carry_back = jax.vjp(carried_in, cumulated, c_state, start_state)
    mixed = (zero_mixed + carried).reshape(rows_here, local_inner)
    gate_act = jax.nn.silu(proj_z)
    gated = mixed * gate_act
    total_sq = lax.psum(jnp.sum(gated * gated, axis=1), "tp")
    gate_rms = lax.rsqrt(total_sq / E + norm_eps)[:, None]
    outnorm = (gated * gate_rms * gate_gain[None, :]).astype(jnp.bfloat16)
    out_part = jnp.dot(outnorm, full_out, preferred_element_type=jnp.float32)
    out_total = lax.psum(out_part, "tp")
    block_out = seq_tokens + out_total
    cotan_b = seq_cotan.astype(jnp.bfloat16)
    grad_norm_out = jnp.einsum("td,ed->te", cotan_b, full_out, preferred_element_type=jnp.float32)
    grad_w_out = jnp.einsum("td,te->de", cotan_b, outnorm, preferred_element_type=jnp.float32)
    inner_sum = lax.psum(jnp.sum(grad_norm_out * gate_gain[None, :] * gated, axis=1), "tp")
    grad_gate_gain = jnp.sum(grad_norm_out * gated * gate_rms, axis=0)
    grad_gated = (
        gate_rms * gate_gain[None, :] * grad_norm_out - gated * gate_rms**3 * inner_sum[:, None] / E
    )
    grad_mixed = (grad_gated * gate_act).reshape(rows_here, local_heads, local_inner // local_heads)
    sigmoid_z = jax.nn.sigmoid(proj_z)
    grad_z = grad_gated * mixed * sigmoid_z * (1.0 + proj_z * (1.0 - sigmoid_z))
    grad_cum, grad_c_carry, grad_start = carry_back(grad_mixed)
    later_decay, grad_next = entering(
        (decay_dev, grad_start), "ctx", chain_link, (chain_ones, chain_zero), True
    )
    grad_decay = jnp.sum(grad_next * start_state, axis=(1, 2))
    grad_x, grad_b, grad_c, grad_dt, grad_step_bias, grad_rate_log, grad_skip = mixer_back(
        (grad_mixed, grad_next, grad_decay, grad_cum)
    )
    grad_c = grad_c + grad_c_carry
    grad_pad, grad_conv_w, grad_conv_b = conv_back(
        jnp.concatenate([grad_x, grad_b, grad_c], axis=1)
    )
    rim_grad = shifted(grad_pad[:taps_less], "ctx", -1)
    grad_pre = grad_pad[taps_less:]
    grad_pre = jnp.concatenate(
        [grad_pre[: rows_here - taps_less], grad_pre[rows_here - taps_less :] + rim_grad], axis=0
    )
    grad_split = jnp.concatenate([grad_z, grad_pre[:, :local_inner], grad_dt], axis=1).astype(
        jnp.bfloat16
    )
    hidden_part = jnp.einsum("tc,dc->td", grad_split, w_split, preferred_element_type=jnp.float32)
    hidden_sum, grad_bc_pre, conv_bc_gw, conv_bc_gb = lax.psum(
        (
            hidden_part,
            grad_pre[:, local_inner:],
            grad_conv_w[:, local_inner:],
            grad_conv_b[local_inner:],
        ),
        "tp",
    )
    grad_bc = grad_bc_pre.astype(jnp.bfloat16)
    grad_hidden = hidden_sum + jnp.einsum(
        "tc,dc->td", grad_bc, full_bc, preferred_element_type=jnp.float32
    )
    grad_norm_gain = jnp.sum(grad_hidden * seq_tokens * inv_rms, axis=0)
    inner_in = jnp.mean(grad_hidden * norm_gain[None, :] * seq_tokens, axis=1, keepdims=True)
    grad_tokens = (
        seq_cotan + inv_rms * norm_gain[None, :] * grad_hidden - seq_tokens * inv_rms**3 * inner_in
    )
    tp_here = lax.axis_index("tp")
    half_bc = lax.dynamic_slice_in_dim(grad_bc, tp_here * state_size, state_size, axis=1)
    in_width = grad_split.shape[1]
    spare = jnp.zeros((rows_here, -in_width % lane), jnp.bfloat16)
    grad_cols = jnp.concatenate([grad_split, spare, half_bc], axis=1)
    grad_w_in = jnp.einsum("td,tc->dc", normed, grad_cols, preferred_element_type=jnp.float32)
    split_grad = jnp.concatenate(
        [
            grad_conv_w[:, :local_inner].reshape(-1),
            grad_conv_b[:local_inner],
            grad_gate_gain,
            grad_step_bias,
            grad_rate_log,
            grad_skip,
        ]
    )[None, :]
    rep_grad = jnp.concatenate([grad_norm_gain, conv_bc_gw.reshape(-1), conv_bc_gb])
    split_size, rep_size = split_grad.shape[1], rep_grad.shape[0]
    small_size = split_size + rep_size
    small = jnp.concatenate(
        [split_grad[0], rep_grad, jnp.zeros((-small_size % (8 * lane),), jnp.float32)]
    ).reshape(-1, lane)
    sum_a, sum_b, sum_pair, sum_small = reduce_grads(grad_w_in, grad_w_out, small)
    summed_in = sum_a[:, None, :in_width]
    mine_bc = sum_a[:, sum_a.shape[1] - state_size :]
    summed_bc = jnp.where(
        tp_here == 0,
        jnp.concatenate([mine_bc, sum_pair], axis=1),
        jnp.concatenate([sum_pair, mine_bc], axis=1),
    )
    summed_out = sum_b.T
    sum_small = sum_small.reshape(-1)
    split_sum = sum_small[:split_size][None, :]
    rep_sum = sum_small[split_size:small_size]
    new_in, new_mom_in = adam_step(mat_in, mom_in, summed_in)
    new_bc, new_mom_bc = adam_step(mat_bc, mom_bc, summed_bc)
    new_out, new_mom_out = adam_step(mat_out, mom_out, summed_out)
    new_split, new_mom_split = adam_step(vec_split, mom_split, split_sum)
    new_rep, new_mom_rep = adam_step(vec_rep, mom_rep, rep_sum)
    return (
        block_out[None],
        grad_tokens[None],
        new_in,
        new_bc,
        new_out,
        new_split,
        new_rep,
        new_mom_in,
        new_mom_bc,
        new_mom_out,
        new_mom_split,
        new_mom_rep,
    )


def solution(mesh):
    return jax.shard_map(
        shards,
        mesh=mesh,
        in_specs=(
            P("dp", "ctx", None),
            P("dp", "ctx", None),
            P("dp", "tp", None),
            P("dp", None),
            P("tp", "dp"),
            P("tp", None),
            P(),
            P(None, "dp", "tp", None),
            P(None, "dp", None),
            P(None, "tp", "dp"),
            P(None, "tp", None),
            P(),
        ),
        out_specs=(
            P("dp", "ctx", None),
            P("dp", "ctx", None),
            P("dp", "tp", None),
            P("dp", None),
            P("tp", "dp"),
            P("tp", None),
            P(),
            P(None, "dp", "tp", None),
            P(None, "dp", None),
            P(None, "tp", "dp"),
            P(None, "tp", None),
            P(),
        ),
        check_vma=False,
    )
```

```python
import functools

import jax
import jax.numpy as jnp
from jax import lax
from jax.experimental import pallas as pl
from jax.experimental.pallas import tpu as pltpu
from jax.sharding import PartitionSpec as P

D = 768
KC = 4
E = 1536


norm_eps = 1e-05
adam_beta1 = 0.9
adam_beta2 = 0.999
adam_eps = 1e-08
learn_rate = 0.01
decay_rate = 0.1
adam_count = 2.0
top_precision = lax.Precision.HIGHEST


def shifted(block, axis, distance):
    devices = range(lax.axis_size(axis))
    route = [(i - distance, i) for i in devices if i - distance in devices]
    return lax.ppermute(block, axis, route)


def collect(decay, state):
    heads, width, depth = state.shape
    tail = jnp.zeros((8, depth), jnp.float32).at[0, :heads].set(decay)
    packed = jnp.concatenate([state.reshape(heads * width, depth), tail], axis=0)
    pieces = lax.all_gather(packed, "ctx")
    states = pieces[:, : heads * width].reshape((-1,) + state.shape)
    return pieces[:, heads * width, :heads], states


def entering(decays, states, axis, backward):
    count, mine = (lax.axis_size(axis), lax.axis_index(axis))
    subtotal = jnp.zeros_like(states[0])
    order = range(count - 1, 0, -1) if backward else range(count - 1)
    for place in order:
        longer = subtotal * decays[place][:, None, None] + states[place]
        keep = place > mine if backward else place < mine
        subtotal = jnp.where(keep, longer, subtotal)
    return subtotal


def conv_apply(padded, weights, biases):
    tap_count = weights.shape[0]
    length = padded.shape[0] - tap_count + 1
    summed = jnp.zeros((length, padded.shape[1]), jnp.float32) + biases[None, :]
    for offset in range(tap_count):
        summed = summed + weights[offset][None, :] * padded[offset : offset + length]
    return jax.nn.silu(summed)


def span_terms(x_heads, b_state, c_state, dt_heads, neg_rates, state_in):
    length = x_heads.shape[0]
    cumulated = jnp.cumsum(dt_heads * neg_rates[None, :], axis=0)
    cum_heads = cumulated.T
    row_pos = lax.broadcasted_iota(jnp.int32, (length, length), 0)
    col_pos = lax.broadcasted_iota(jnp.int32, (length, length), 1)
    causal = (col_pos <= row_pos)[None, :, :]
    differ = cum_heads[:, :, None] - cum_heads[:, None, :]
    decays = jnp.where(causal, jnp.exp(jnp.where(causal, differ, 0.0)), 0.0)
    scores = jnp.dot(c_state, b_state.T, precision=top_precision)
    mixing = scores[None, :, :] * decays * dt_heads.T[:, None, :]
    inside = jnp.einsum("hts,shp->thp", mixing, x_heads, precision=top_precision)
    carried = jnp.exp(cumulated)[:, :, None] * jnp.einsum(
        "tn,hpn->thp", c_state, state_in, precision=top_precision
    )
    ending = cumulated[-1]
    weights_tail = jnp.exp(ending[None, :] - cumulated) * dt_heads
    state_out = jnp.exp(ending)[:, None, None] * state_in + jnp.einsum(
        "sh,shp,sn->hpn", weights_tail, x_heads, b_state, precision=top_precision
    )
    return (inside + carried, state_out)


def local_mixer(x_cols, b_state, c_state, dt_raw, step_bias, rate_log, skip_gain):
    rows_here = x_cols.shape[0]
    head_count = dt_raw.shape[1]
    head_width = x_cols.shape[1] // head_count
    steps_dt = jax.nn.softplus(dt_raw + step_bias[None, :])
    neg_rates = -jnp.exp(rate_log)
    x_heads = x_cols.reshape(rows_here, head_count, head_width)
    state_now = jnp.zeros((head_count, head_width, b_state.shape[1]), jnp.float32)
    part_out, state_now = span_terms(x_heads, b_state, c_state, steps_dt, neg_rates, state_now)
    pieces = [part_out]
    cumulated = jnp.cumsum(steps_dt * neg_rates[None, :], axis=0)
    mixed = jnp.concatenate(pieces, axis=0) + skip_gain[None, :, None] * x_heads
    return (mixed, state_now, jnp.exp(cumulated[-1]), cumulated)


def carried_in(cumulated, c_state, start_state):
    return jnp.exp(cumulated)[:, :, None] * jnp.einsum(
        "tn,hpn->thp", c_state, start_state, precision=top_precision
    )


lane = 128
chunk_lanes = 4
mesh_ids = pl.DeviceIdType.MESH


def greet(peers):
    barrier = pltpu.get_barrier_semaphore()
    for peer in peers:
        pl.semaphore_signal(barrier, inc=1, device_id=peer, device_id_type=mesh_ids)
    pl.semaphore_wait(barrier, len(peers))


def others(axis, count):
    mine = lax.axis_index(axis)
    return [lax.rem(mine + step, count) for step in range(1, count)]


def send(src, dst, sent, got, axis, peer):
    copy = pltpu.make_async_remote_copy(
        src_ref=src,
        dst_ref=dst,
        send_sem=sent,
        recv_sem=got,
        device_id={axis: peer},
        device_id_type=mesh_ids,
    )
    copy.start()
    return copy


def back_body(count, rows_ref, out_ref, slot, sent, got):
    here = lax.axis_index("ctx")
    left, right = lax.rem(here + count - 1, count), lax.rem(here + 1, count)
    greet([{"ctx": left}, {"ctx": right}])
    copy = send(rows_ref, slot, sent, got, "ctx", left)
    copy.wait()
    out_ref[...] = slot[...]


def shift_back(rows):
    count = lax.axis_size("ctx")
    vmem = pl.BlockSpec(memory_space=pltpu.VMEM)
    moved = pl.pallas_call(
        functools.partial(back_body, count),
        out_shape=jax.ShapeDtypeStruct(rows.shape, rows.dtype),
        in_specs=[vmem],
        out_specs=vmem,
        scratch_shapes=[
            pltpu.VMEM(rows.shape, rows.dtype),
            pltpu.SemaphoreType.DMA,
            pltpu.SemaphoreType.DMA,
        ],
        compiler_params=pltpu.CompilerParams(collective_id=1, has_side_effects=True),
        name="shift_back",
    )(rows)
    return jnp.where(lax.axis_index("ctx") < count - 1, moved, 0.0)


def column_chunks(width):
    step = chunk_lanes * lane
    return [(at, min(step, width - at)) for at in range(0, width, step)]


def reduce_body(
    dp_count, ctx_count, a_ref, b_ref, s_ref, out_a, out_b, out_pair, out_s,
    slot_a, slot_b, red_a, red_b, zslot_a, zslot_b, all_a, all_b, pair_slot,
    s_slot, s_red, s_zslot,
    sent1, got1, sent2, got2, sent3, got3, s_sent, s_got, pair_sent, pair_got,
):
    me = lax.axis_index("dp")
    here = lax.axis_index("ctx")
    dp_peers = others("dp", dp_count)
    ctx_peers = others("ctx", ctx_count)
    partner = 1 - lax.axis_index("tp")
    greet(
        [{"dp": peer} for peer in dp_peers]
        + [{"ctx": peer} for peer in ctx_peers]
        + [{"tp": partner}]
    )
    wide = a_ref.shape[3]
    half = wide - lane
    chunks = [(0, half, lane)]
    chunks += [(0, at, size) for at, size in column_chunks(half)]
    chunks += [(1, at, size) for at, size in column_chunks(b_ref.shape[3])]
    sources = (a_ref, b_ref)
    slots, reds, zslots, alls = (slot_a, slot_b), (red_a, red_b), (zslot_a, zslot_b), (all_a, all_b)
    waits = []

    s_copies = []
    for step, peer in enumerate(dp_peers):
        s_copies.append(send(s_ref, s_slot.at[me], s_sent.at[0, step], s_got.at[0, step], "dp", peer))
    first = []
    for number, (which, at, size) in enumerate(chunks):
        cols = pl.ds(at, size)
        first.append([
            send(
                sources[which].at[peer, :, :, cols],
                slots[which].at[step, :, :, cols],
                sent1.at[number, step],
                got1.at[number, step],
                "dp",
                peer,
            )
            for step, peer in enumerate(dp_peers)
        ])
    s_slot[me] = s_ref[...]
    for copy in s_copies:
        copy.wait_recv()
    total = s_slot[0]
    for step in range(1, dp_count):
        total = total + s_slot[step]
    s_red[...] = total
    s_zslot[here] = total
    z_copies = []
    for step, peer in enumerate(ctx_peers):
        z_copies.append(
            send(s_red, s_zslot.at[here], s_sent.at[1, step], s_got.at[1, step], "ctx", peer)
        )
    waits += s_copies + z_copies

    second = []
    third = []

    def scatter(number):
        which, at, size = chunks[number]
        cols = pl.ds(at, size)
        for copy in first[number]:
            copy.wait_recv()
        total = sources[which][me, :, :, cols]
        for step in range(dp_count - 1):
            total = total + slots[which][step, :, :, cols]
        reds[which][:, :, cols] = total
        second.append([
            send(
                reds[which].at[peer, :, cols],
                zslots[which].at[step, :, cols],
                sent2.at[number, step],
                got2.at[number, step],
                "ctx",
                peer,
            )
            for step, peer in enumerate(ctx_peers)
        ])

    def gather(number):
        which, at, size = chunks[number]
        cols = pl.ds(at, size)
        for copy in second[number]:
            copy.wait_recv()
        total = reds[which][here, :, cols]
        for step in range(ctx_count - 1):
            total = total + zslots[which][step, :, cols]
        alls[which][here, :, cols] = total
        third.append([
            send(
                alls[which].at[here, :, cols],
                alls[which].at[here, :, cols],
                sent3.at[number, step],
                got3.at[number, step],
                "ctx",
                peer,
            )
            for step, peer in enumerate(ctx_peers)
        ])

    def exchange():
        for copy in third[0]:
            copy.wait_recv()
        return send(
            all_a.at[:, :, pl.ds(half, lane)], pair_slot, pair_sent, pair_got, "tp", partner
        )

    pair = None
    for number in range(len(chunks) + 1):
        if number < len(chunks):
            scatter(number)
        if number >= 1:
            gather(number - 1)
        if number == 2:
            pair = exchange()
    for copy in z_copies:
        copy.wait_recv()
    total = s_zslot[0]
    for step in range(1, ctx_count):
        total = total + s_zslot[step]
    out_s[...] = total
    outs = (out_a, out_b)
    for number, (which, at, size) in enumerate(chunks):
        cols = pl.ds(at, size)
        if number > 0:
            for copy in third[number]:
                copy.wait_recv()
        outs[which][:, :, cols] = alls[which][:, :, cols]
    pair.wait_recv()
    out_pair[...] = pair_slot[...]
    pair.wait_send()
    for group in first + second + third + [waits]:
        for copy in group:
            copy.wait_send()


def reduce_grads(grad_a, grad_b, small):
    dp_count, ctx_count = lax.axis_size("dp"), lax.axis_size("ctx")
    rows = grad_a.shape[0] // (dp_count * ctx_count)
    wide_a, wide_b = grad_a.shape[1], grad_b.shape[1]
    count = 1 + len(column_chunks(wide_a - lane)) + len(column_chunks(wide_b))
    f32 = jnp.float32
    vmem = pl.BlockSpec(memory_space=pltpu.VMEM)
    semaphores = [
        pltpu.SemaphoreType.DMA((count, dp_count - 1)),
        pltpu.SemaphoreType.DMA((count, dp_count - 1)),
        pltpu.SemaphoreType.DMA((count, ctx_count - 1)),
        pltpu.SemaphoreType.DMA((count, ctx_count - 1)),
        pltpu.SemaphoreType.DMA((count, ctx_count - 1)),
        pltpu.SemaphoreType.DMA((count, ctx_count - 1)),
        pltpu.SemaphoreType.DMA((2, max(dp_count, ctx_count))),
        pltpu.SemaphoreType.DMA((2, max(dp_count, ctx_count))),
        pltpu.SemaphoreType.DMA,
        pltpu.SemaphoreType.DMA,
    ]
    own_a, own_b = (ctx_count, rows, wide_a), (ctx_count, rows, wide_b)
    out_a, out_b, out_pair, out_s = pl.pallas_call(
        functools.partial(reduce_body, dp_count, ctx_count),
        out_shape=(
            jax.ShapeDtypeStruct(own_a, f32),
            jax.ShapeDtypeStruct(own_b, f32),
            jax.ShapeDtypeStruct((ctx_count, rows, lane), f32),
            jax.ShapeDtypeStruct(small.shape, f32),
        ),
        in_specs=[vmem] * 3,
        out_specs=(vmem,) * 4,
        scratch_shapes=[
            pltpu.VMEM((dp_count - 1,) + own_a, f32),
            pltpu.VMEM((dp_count - 1,) + own_b, f32),
            pltpu.VMEM(own_a, f32),
            pltpu.VMEM(own_b, f32),
            pltpu.VMEM((ctx_count - 1, rows, wide_a), f32),
            pltpu.VMEM((ctx_count - 1, rows, wide_b), f32),
            pltpu.VMEM(own_a, f32),
            pltpu.VMEM(own_b, f32),
            pltpu.VMEM((ctx_count, rows, lane), f32),
            pltpu.VMEM((dp_count,) + small.shape, f32),
            pltpu.VMEM(small.shape, f32),
            pltpu.VMEM((ctx_count,) + small.shape, f32),
        ]
        + semaphores,
        compiler_params=pltpu.CompilerParams(collective_id=0, has_side_effects=True),
        name="reduce_grads",
    )(
        grad_a.reshape((dp_count,) + own_a),
        grad_b.reshape((dp_count,) + own_b),
        small,
    )
    flat = lambda part: part.reshape(ctx_count * rows, part.shape[-1])
    return flat(out_a), flat(out_b), flat(out_pair), out_s


def adam_step(weights, moments, grads):
    first_mom = adam_beta1 * moments[0] + (1.0 - adam_beta1) * grads
    second_mom = adam_beta2 * moments[1] + (1.0 - adam_beta2) * grads * grads
    first_hat = first_mom / (1.0 - adam_beta1**adam_count)
    second_hat = second_mom / (1.0 - adam_beta2**adam_count)
    updated = weights - learn_rate * (
        first_hat / (jnp.sqrt(second_hat) + adam_eps) + decay_rate * weights
    )
    return (updated, jnp.stack([first_mom, second_mom]))


def shards(
    tokens,
    cotangent,
    mat_in,
    mat_bc,
    mat_out,
    vec_split,
    vec_rep,
    mom_in,
    mom_bc,
    mom_out,
    mom_split,
    mom_rep,
):
    full_in, full_bc, full_out = (
        lax.all_gather(mat_in.astype(jnp.bfloat16), "dp", axis=0, tiled=True),
        lax.all_gather(mat_bc.astype(jnp.bfloat16), "dp", axis=0, tiled=True),
        lax.all_gather(mat_out.astype(jnp.bfloat16), "dp", axis=1, tiled=True),
    )
    w_split = full_in[:, 0, :]
    local_inner = full_out.shape[0]
    local_heads = w_split.shape[1] - 2 * local_inner
    state_size = full_bc.shape[1] // 2
    taps_less = KC - 1
    seq_tokens = tokens[0]
    seq_cotan = cotangent[0]
    rows_here = seq_tokens.shape[0]
    split_row = vec_split[0]
    conv_x_w = split_row[: KC * local_inner].reshape(KC, local_inner)
    conv_end = KC * local_inner
    conv_x_b = split_row[conv_end : conv_end + local_inner]
    gate_gain = split_row[conv_end + local_inner : conv_end + 2 * local_inner]
    head_base = conv_end + 2 * local_inner
    step_bias = split_row[head_base : head_base + local_heads]
    rate_log = split_row[head_base + local_heads : head_base + 2 * local_heads]
    skip_gain = split_row[head_base + 2 * local_heads :]
    norm_gain = vec_rep[:D]
    conv_bc_w = vec_rep[D : D + KC * 2 * state_size].reshape(KC, 2 * state_size)
    conv_bc_b = vec_rep[D + KC * 2 * state_size :]
    conv_all_w = jnp.concatenate([conv_x_w, conv_bc_w], axis=1)
    conv_all_b = jnp.concatenate([conv_x_b, conv_bc_b])
    inv_rms = lax.rsqrt(jnp.mean(seq_tokens * seq_tokens, axis=1, keepdims=True) + norm_eps)
    normed = (seq_tokens * inv_rms * norm_gain[None, :]).astype(jnp.bfloat16)
    rim_tokens = shifted(seq_tokens[rows_here - taps_less :], "ctx", 1)
    rim_rms = lax.rsqrt(jnp.mean(rim_tokens * rim_tokens, axis=1, keepdims=True) + norm_eps)
    rim_normed = (rim_tokens * rim_rms * norm_gain[None, :]).astype(jnp.bfloat16)
    rim_normed = jnp.concatenate([rim_normed, jnp.zeros((16 - taps_less, D), jnp.bfloat16)], axis=0)
    proj_split = jnp.dot(normed, w_split, preferred_element_type=jnp.float32)
    proj_bc = jnp.dot(normed, full_bc, preferred_element_type=jnp.float32)
    proj_z = proj_split[:, :local_inner]
    proj_dt = proj_split[:, 2 * local_inner :]
    pre_conv = jnp.concatenate([proj_split[:, local_inner : 2 * local_inner], proj_bc], axis=1)
    rim_rows = jnp.concatenate(
        [
            jnp.dot(
                rim_normed,
                w_split[:, local_inner : 2 * local_inner],
                preferred_element_type=jnp.float32,
            ),
            jnp.dot(rim_normed, full_bc, preferred_element_type=jnp.float32),
        ],
        axis=1,
    )[:taps_less]
    padded = jnp.concatenate([rim_rows, pre_conv], axis=0)
    activated, conv_back = jax.vjp(conv_apply, padded, conv_all_w, conv_all_b)
    x_cols = activated[:, :local_inner]
    b_state = activated[:, local_inner : local_inner + state_size]
    c_state = activated[:, local_inner + state_size :]
    mixer_out, mixer_back = jax.vjp(
        local_mixer, x_cols, b_state, c_state, proj_dt, step_bias, rate_log, skip_gain
    )
    zero_mixed, local_state, decay_dev, cumulated = mixer_out
    decays, states = collect(decay_dev, local_state)
    start_state = entering(decays, states, "ctx", False)
    carried, carry_back = jax.vjp(carried_in, cumulated, c_state, start_state)
    mixed = (zero_mixed + carried).reshape(rows_here, local_inner)
    gate_act = jax.nn.silu(proj_z)
    gated = mixed * gate_act
    total_sq = lax.psum(jnp.sum(gated * gated, axis=1), "tp")
    gate_rms = lax.rsqrt(total_sq / E + norm_eps)[:, None]
    outnorm = (gated * gate_rms * gate_gain[None, :]).astype(jnp.bfloat16)
    out_part = jnp.dot(outnorm, full_out, preferred_element_type=jnp.float32)
    out_total = lax.psum(out_part, "tp")
    block_out = seq_tokens + out_total
    cotan_b = seq_cotan.astype(jnp.bfloat16)
    grad_norm_out = jnp.einsum("td,ed->te", cotan_b, full_out, preferred_element_type=jnp.float32)
    grad_w_out = jnp.einsum("td,te->de", cotan_b, outnorm, preferred_element_type=jnp.float32)
    inner_sum = lax.psum(jnp.sum(grad_norm_out * gate_gain[None, :] * gated, axis=1), "tp")
    grad_gate_gain = jnp.sum(grad_norm_out * gated * gate_rms, axis=0)
    grad_gated = (
        gate_rms * gate_gain[None, :] * grad_norm_out - gated * gate_rms**3 * inner_sum[:, None] / E
    )
    grad_mixed = (grad_gated * gate_act).reshape(rows_here, local_heads, local_inner // local_heads)
    sigmoid_z = jax.nn.sigmoid(proj_z)
    grad_z = grad_gated * mixed * sigmoid_z * (1.0 + proj_z * (1.0 - sigmoid_z))
    grad_cum, grad_c_carry, grad_start = carry_back(grad_mixed)
    grad_next = entering(decays, lax.all_gather(grad_start, "ctx"), "ctx", True)
    grad_decay = jnp.sum(grad_next * start_state, axis=(1, 2))
    grad_x, grad_b, grad_c, grad_dt, grad_step_bias, grad_rate_log, grad_skip = mixer_back(
        (grad_mixed, grad_next, grad_decay, grad_cum)
    )
    grad_c = grad_c + grad_c_carry
    grad_pad, grad_conv_w, grad_conv_b = conv_back(
        jnp.concatenate([grad_x, grad_b, grad_c], axis=1)
    )
    rim_grad = shift_back(grad_pad[:8])[:taps_less]
    grad_pre = grad_pad[taps_less:]
    grad_pre = jnp.concatenate(
        [grad_pre[: rows_here - taps_less], grad_pre[rows_here - taps_less :] + rim_grad], axis=0
    )
    grad_split = jnp.concatenate([grad_z, grad_pre[:, :local_inner], grad_dt], axis=1).astype(
        jnp.bfloat16
    )
    hidden_part = jnp.einsum("tc,dc->td", grad_split, w_split, preferred_element_type=jnp.float32)
    hidden_sum, grad_bc_pre, conv_bc_gw, conv_bc_gb = lax.psum(
        (
            hidden_part,
            grad_pre[:, local_inner:],
            grad_conv_w[:, local_inner:],
            grad_conv_b[local_inner:],
        ),
        "tp",
    )
    grad_bc = grad_bc_pre.astype(jnp.bfloat16)
    grad_hidden = hidden_sum + jnp.einsum(
        "tc,dc->td", grad_bc, full_bc, preferred_element_type=jnp.float32
    )
    grad_norm_gain = jnp.sum(grad_hidden * seq_tokens * inv_rms, axis=0)
    inner_in = jnp.mean(grad_hidden * norm_gain[None, :] * seq_tokens, axis=1, keepdims=True)
    grad_tokens = (
        seq_cotan + inv_rms * norm_gain[None, :] * grad_hidden - seq_tokens * inv_rms**3 * inner_in
    )
    tp_here = lax.axis_index("tp")
    half_bc = lax.dynamic_slice_in_dim(grad_bc, tp_here * state_size, state_size, axis=1)
    in_width = grad_split.shape[1]
    spare = jnp.zeros((rows_here, -in_width % lane), jnp.bfloat16)
    grad_cols = jnp.concatenate([grad_split, spare, half_bc], axis=1)
    grad_w_in = jnp.einsum("td,tc->dc", normed, grad_cols, preferred_element_type=jnp.float32)
    split_grad = jnp.concatenate(
        [
            grad_conv_w[:, :local_inner].reshape(-1),
            grad_conv_b[:local_inner],
            grad_gate_gain,
            grad_step_bias,
            grad_rate_log,
            grad_skip,
        ]
    )[None, :]
    rep_grad = jnp.concatenate([grad_norm_gain, conv_bc_gw.reshape(-1), conv_bc_gb])
    split_size, rep_size = split_grad.shape[1], rep_grad.shape[0]
    small_size = split_size + rep_size
    small = jnp.concatenate(
        [split_grad[0], rep_grad, jnp.zeros((-small_size % (8 * lane),), jnp.float32)]
    ).reshape(-1, lane)
    sum_a, sum_b, sum_pair, sum_small = reduce_grads(grad_w_in, grad_w_out, small)
    summed_in = sum_a[:, None, :in_width]
    mine_bc = sum_a[:, sum_a.shape[1] - state_size :]
    summed_bc = jnp.where(
        tp_here == 0,
        jnp.concatenate([mine_bc, sum_pair], axis=1),
        jnp.concatenate([sum_pair, mine_bc], axis=1),
    )
    summed_out = sum_b.T
    sum_small = sum_small.reshape(-1)
    split_sum = sum_small[:split_size][None, :]
    rep_sum = sum_small[split_size:small_size]
    new_in, new_mom_in = adam_step(mat_in, mom_in, summed_in)
    new_bc, new_mom_bc = adam_step(mat_bc, mom_bc, summed_bc)
    new_out, new_mom_out = adam_step(mat_out, mom_out, summed_out)
    new_split, new_mom_split = adam_step(vec_split, mom_split, split_sum)
    new_rep, new_mom_rep = adam_step(vec_rep, mom_rep, rep_sum)
    return (
        block_out[None],
        grad_tokens[None],
        new_in,
        new_bc,
        new_out,
        new_split,
        new_rep,
        new_mom_in,
        new_mom_bc,
        new_mom_out,
        new_mom_split,
        new_mom_rep,
    )


def solution(mesh):
    return jax.shard_map(
        shards,
        mesh=mesh,
        in_specs=(
            P("dp", "ctx", None),
            P("dp", "ctx", None),
            P("dp", "tp", None),
            P("dp", None),
            P("tp", "dp"),
            P("tp", None),
            P(),
            P(None, "dp", "tp", None),
            P(None, "dp", None),
            P(None, "tp", "dp"),
            P(None, "tp", None),
            P(),
        ),
        out_specs=(
            P("dp", "ctx", None),
            P("dp", "ctx", None),
            P("dp", "tp", None),
            P("dp", None),
            P("tp", "dp"),
            P("tp", None),
            P(),
            P(None, "dp", "tp", None),
            P(None, "dp", None),
            P(None, "tp", "dp"),
            P(None, "tp", None),
            P(),
        ),
        check_vma=False,
    )
```

```python
import functools

import jax
import jax.numpy as jnp
from jax import lax
from jax.experimental import pallas as pl
from jax.experimental.pallas import tpu as pltpu
from jax.sharding import PartitionSpec as P

D = 768
KC = 4
E = 1536


norm_eps = 1e-05
adam_beta1 = 0.9
adam_beta2 = 0.999
adam_eps = 1e-08
learn_rate = 0.01
decay_rate = 0.1
adam_count = 2.0
top_precision = lax.Precision.HIGHEST


def shifted(block, axis, distance):
    devices = range(lax.axis_size(axis))
    route = [(i - distance, i) for i in devices if i - distance in devices]
    return lax.ppermute(block, axis, route)


def collect(decay, state):
    heads, width, depth = state.shape
    tail = jnp.zeros((8, depth), jnp.float32).at[0, :heads].set(decay)
    packed = jnp.concatenate([state.reshape(heads * width, depth), tail], axis=0)
    pieces = lax.all_gather(packed, "ctx")
    states = pieces[:, : heads * width].reshape((-1,) + state.shape)
    return pieces[:, heads * width, :heads], states


def entering(decays, states, axis, backward):
    count, mine = (lax.axis_size(axis), lax.axis_index(axis))
    subtotal = jnp.zeros_like(states[0])
    order = range(count - 1, 0, -1) if backward else range(count - 1)
    for place in order:
        longer = subtotal * decays[place][:, None, None] + states[place]
        keep = place > mine if backward else place < mine
        subtotal = jnp.where(keep, longer, subtotal)
    return subtotal


def conv_apply(padded, weights, biases):
    tap_count = weights.shape[0]
    length = padded.shape[0] - tap_count + 1
    summed = jnp.zeros((length, padded.shape[1]), jnp.float32) + biases[None, :]
    for offset in range(tap_count):
        summed = summed + weights[offset][None, :] * padded[offset : offset + length]
    return jax.nn.silu(summed)


def span_terms(x_heads, b_state, c_state, dt_heads, neg_rates, state_in):
    length = x_heads.shape[0]
    cumulated = jnp.cumsum(dt_heads * neg_rates[None, :], axis=0)
    cum_heads = cumulated.T
    row_pos = lax.broadcasted_iota(jnp.int32, (length, length), 0)
    col_pos = lax.broadcasted_iota(jnp.int32, (length, length), 1)
    causal = (col_pos <= row_pos)[None, :, :]
    differ = cum_heads[:, :, None] - cum_heads[:, None, :]
    decays = jnp.where(causal, jnp.exp(jnp.where(causal, differ, 0.0)), 0.0)
    scores = jnp.dot(c_state, b_state.T, precision=top_precision)
    mixing = scores[None, :, :] * decays * dt_heads.T[:, None, :]
    inside = jnp.einsum("hts,shp->thp", mixing, x_heads, precision=top_precision)
    carried = jnp.exp(cumulated)[:, :, None] * jnp.einsum(
        "tn,hpn->thp", c_state, state_in, precision=top_precision
    )
    ending = cumulated[-1]
    weights_tail = jnp.exp(ending[None, :] - cumulated) * dt_heads
    state_out = jnp.exp(ending)[:, None, None] * state_in + jnp.einsum(
        "sh,shp,sn->hpn", weights_tail, x_heads, b_state, precision=top_precision
    )
    return (inside + carried, state_out)


def local_mixer(x_cols, b_state, c_state, dt_raw, step_bias, rate_log, skip_gain):
    rows_here = x_cols.shape[0]
    head_count = dt_raw.shape[1]
    head_width = x_cols.shape[1] // head_count
    steps_dt = jax.nn.softplus(dt_raw + step_bias[None, :])
    neg_rates = -jnp.exp(rate_log)
    x_heads = x_cols.reshape(rows_here, head_count, head_width)
    state_now = jnp.zeros((head_count, head_width, b_state.shape[1]), jnp.float32)
    part_out, state_now = span_terms(x_heads, b_state, c_state, steps_dt, neg_rates, state_now)
    pieces = [part_out]
    cumulated = jnp.cumsum(steps_dt * neg_rates[None, :], axis=0)
    mixed = jnp.concatenate(pieces, axis=0) + skip_gain[None, :, None] * x_heads
    return (mixed, state_now, jnp.exp(cumulated[-1]), cumulated)


def carried_in(cumulated, c_state, start_state):
    return jnp.exp(cumulated)[:, :, None] * jnp.einsum(
        "tn,hpn->thp", c_state, start_state, precision=top_precision
    )


lane = 128
chunk_lanes = 2
mesh_ids = pl.DeviceIdType.MESH


def greet(peers):
    barrier = pltpu.get_barrier_semaphore()
    for peer in peers:
        pl.semaphore_signal(barrier, inc=1, device_id=peer, device_id_type=mesh_ids)
    pl.semaphore_wait(barrier, len(peers))


def others(axis, count):
    mine = lax.axis_index(axis)
    return [lax.rem(mine + step, count) for step in range(1, count)]


def send(src, dst, sent, got, axis, peer):
    copy = pltpu.make_async_remote_copy(
        src_ref=src,
        dst_ref=dst,
        send_sem=sent,
        recv_sem=got,
        device_id={axis: peer},
        device_id_type=mesh_ids,
    )
    copy.start()
    return copy


def back_body(count, rows_ref, out_ref, slot, sent, got):
    here = lax.axis_index("ctx")
    left, right = lax.rem(here + count - 1, count), lax.rem(here + 1, count)
    greet([{"ctx": left}, {"ctx": right}])
    copy = send(rows_ref, slot, sent, got, "ctx", left)
    copy.wait()
    out_ref[...] = slot[...]


def shift_back(rows):
    count = lax.axis_size("ctx")
    vmem = pl.BlockSpec(memory_space=pltpu.VMEM)
    moved = pl.pallas_call(
        functools.partial(back_body, count),
        out_shape=jax.ShapeDtypeStruct(rows.shape, rows.dtype),
        in_specs=[vmem],
        out_specs=vmem,
        scratch_shapes=[
            pltpu.VMEM(rows.shape, rows.dtype),
            pltpu.SemaphoreType.DMA,
            pltpu.SemaphoreType.DMA,
        ],
        compiler_params=pltpu.CompilerParams(collective_id=1, has_side_effects=True),
        name="shift_back",
    )(rows)
    return jnp.where(lax.axis_index("ctx") < count - 1, moved, 0.0)


def column_chunks(width):
    step = chunk_lanes * lane
    return [(at, min(step, width - at)) for at in range(0, width, step)]


def reduce_body(
    dp_count, ctx_count, a_ref, b_ref, s_ref, out_a, out_b, out_pair, out_s,
    slot_a, slot_b, red_a, red_b, zslot_a, zslot_b, all_a, all_b, pair_slot,
    s_slot, s_red, s_zslot,
    sent1, got1, sent2, got2, sent3, got3, s_sent, s_got, pair_sent, pair_got,
):
    me = lax.axis_index("dp")
    here = lax.axis_index("ctx")
    dp_peers = others("dp", dp_count)
    ctx_peers = others("ctx", ctx_count)
    partner = 1 - lax.axis_index("tp")
    greet(
        [{"dp": peer} for peer in dp_peers]
        + [{"ctx": peer} for peer in ctx_peers]
        + [{"tp": partner}]
    )
    wide = a_ref.shape[3]
    half = wide - lane
    chunks = [(0, half, lane)]
    chunks += [(0, at, size) for at, size in column_chunks(half)]
    chunks += [(1, at, size) for at, size in column_chunks(b_ref.shape[3])]
    sources = (a_ref, b_ref)
    slots, reds, zslots, alls = (slot_a, slot_b), (red_a, red_b), (zslot_a, zslot_b), (all_a, all_b)
    waits = []

    s_copies = []
    for step, peer in enumerate(dp_peers):
        s_copies.append(send(s_ref, s_slot.at[me], s_sent.at[0, step], s_got.at[0, step], "dp", peer))
    first = []
    for number, (which, at, size) in enumerate(chunks):
        cols = pl.ds(at, size)
        first.append([
            send(
                sources[which].at[peer, :, :, cols],
                slots[which].at[step, :, :, cols],
                sent1.at[number, step],
                got1.at[number, step],
                "dp",
                peer,
            )
            for step, peer in enumerate(dp_peers)
        ])
    s_slot[me] = s_ref[...]
    for copy in s_copies:
        copy.wait_recv()
    total = s_slot[0]
    for step in range(1, dp_count):
        total = total + s_slot[step]
    s_red[...] = total
    s_zslot[here] = total
    z_copies = []
    for step, peer in enumerate(ctx_peers):
        z_copies.append(
            send(s_red, s_zslot.at[here], s_sent.at[1, step], s_got.at[1, step], "ctx", peer)
        )
    waits += s_copies + z_copies

    second = []
    third = []

    def scatter(number):
        which, at, size = chunks[number]
        cols = pl.ds(at, size)
        for copy in first[number]:
            copy.wait_recv()
        total = sources[which][me, :, :, cols]
        for step in range(dp_count - 1):
            total = total + slots[which][step, :, :, cols]
        reds[which][:, :, cols] = total
        second.append([
            send(
                reds[which].at[peer, :, cols],
                zslots[which].at[step, :, cols],
                sent2.at[number, step],
                got2.at[number, step],
                "ctx",
                peer,
            )
            for step, peer in enumerate(ctx_peers)
        ])

    def gather(number):
        which, at, size = chunks[number]
        cols = pl.ds(at, size)
        for copy in second[number]:
            copy.wait_recv()
        total = reds[which][here, :, cols]
        for step in range(ctx_count - 1):
            total = total + zslots[which][step, :, cols]
        alls[which][here, :, cols] = total
        third.append([
            send(
                alls[which].at[here, :, cols],
                alls[which].at[here, :, cols],
                sent3.at[number, step],
                got3.at[number, step],
                "ctx",
                peer,
            )
            for step, peer in enumerate(ctx_peers)
        ])

    def exchange():
        for copy in third[0]:
            copy.wait_recv()
        return send(
            all_a.at[:, :, pl.ds(half, lane)], pair_slot, pair_sent, pair_got, "tp", partner
        )

    pair = None
    for number in range(len(chunks) + 1):
        if number < len(chunks):
            scatter(number)
        if number >= 1:
            gather(number - 1)
        if number == 2:
            pair = exchange()
    for copy in z_copies:
        copy.wait_recv()
    total = s_zslot[0]
    for step in range(1, ctx_count):
        total = total + s_zslot[step]
    out_s[...] = total
    outs = (out_a, out_b)
    for number, (which, at, size) in enumerate(chunks):
        cols = pl.ds(at, size)
        if number > 0:
            for copy in third[number]:
                copy.wait_recv()
        outs[which][:, :, cols] = alls[which][:, :, cols]
    pair.wait_recv()
    out_pair[...] = pair_slot[...]
    pair.wait_send()
    for group in first + second + third + [waits]:
        for copy in group:
            copy.wait_send()


def reduce_grads(grad_a, grad_b, small):
    dp_count, ctx_count = lax.axis_size("dp"), lax.axis_size("ctx")
    rows = grad_a.shape[0] // (dp_count * ctx_count)
    wide_a, wide_b = grad_a.shape[1], grad_b.shape[1]
    count = 1 + len(column_chunks(wide_a - lane)) + len(column_chunks(wide_b))
    f32 = jnp.float32
    vmem = pl.BlockSpec(memory_space=pltpu.VMEM)
    semaphores = [
        pltpu.SemaphoreType.DMA((count, dp_count - 1)),
        pltpu.SemaphoreType.DMA((count, dp_count - 1)),
        pltpu.SemaphoreType.DMA((count, ctx_count - 1)),
        pltpu.SemaphoreType.DMA((count, ctx_count - 1)),
        pltpu.SemaphoreType.DMA((count, ctx_count - 1)),
        pltpu.SemaphoreType.DMA((count, ctx_count - 1)),
        pltpu.SemaphoreType.DMA((2, max(dp_count, ctx_count))),
        pltpu.SemaphoreType.DMA((2, max(dp_count, ctx_count))),
        pltpu.SemaphoreType.DMA,
        pltpu.SemaphoreType.DMA,
    ]
    own_a, own_b = (ctx_count, rows, wide_a), (ctx_count, rows, wide_b)
    out_a, out_b, out_pair, out_s = pl.pallas_call(
        functools.partial(reduce_body, dp_count, ctx_count),
        out_shape=(
            jax.ShapeDtypeStruct(own_a, f32),
            jax.ShapeDtypeStruct(own_b, f32),
            jax.ShapeDtypeStruct((ctx_count, rows, lane), f32),
            jax.ShapeDtypeStruct(small.shape, f32),
        ),
        in_specs=[vmem] * 3,
        out_specs=(vmem,) * 4,
        scratch_shapes=[
            pltpu.VMEM((dp_count - 1,) + own_a, f32),
            pltpu.VMEM((dp_count - 1,) + own_b, f32),
            pltpu.VMEM(own_a, f32),
            pltpu.VMEM(own_b, f32),
            pltpu.VMEM((ctx_count - 1, rows, wide_a), f32),
            pltpu.VMEM((ctx_count - 1, rows, wide_b), f32),
            pltpu.VMEM(own_a, f32),
            pltpu.VMEM(own_b, f32),
            pltpu.VMEM((ctx_count, rows, lane), f32),
            pltpu.VMEM((dp_count,) + small.shape, f32),
            pltpu.VMEM(small.shape, f32),
            pltpu.VMEM((ctx_count,) + small.shape, f32),
        ]
        + semaphores,
        compiler_params=pltpu.CompilerParams(collective_id=0, has_side_effects=True),
        name="reduce_grads",
    )(
        grad_a.reshape((dp_count,) + own_a),
        grad_b.reshape((dp_count,) + own_b),
        small,
    )
    flat = lambda part: part.reshape(ctx_count * rows, part.shape[-1])
    return flat(out_a), flat(out_b), flat(out_pair), out_s


def adam_step(weights, moments, grads):
    first_mom = adam_beta1 * moments[0] + (1.0 - adam_beta1) * grads
    second_mom = adam_beta2 * moments[1] + (1.0 - adam_beta2) * grads * grads
    first_hat = first_mom / (1.0 - adam_beta1**adam_count)
    second_hat = second_mom / (1.0 - adam_beta2**adam_count)
    updated = weights - learn_rate * (
        first_hat / (jnp.sqrt(second_hat) + adam_eps) + decay_rate * weights
    )
    return (updated, jnp.stack([first_mom, second_mom]))


def shards(
    tokens,
    cotangent,
    mat_in,
    mat_bc,
    mat_out,
    vec_split,
    vec_rep,
    mom_in,
    mom_bc,
    mom_out,
    mom_split,
    mom_rep,
):
    full_in, full_bc, full_out = (
        lax.all_gather(mat_in.astype(jnp.bfloat16), "dp", axis=0, tiled=True),
        lax.all_gather(mat_bc.astype(jnp.bfloat16), "dp", axis=0, tiled=True),
        lax.all_gather(mat_out.astype(jnp.bfloat16), "dp", axis=1, tiled=True),
    )
    w_split = full_in[:, 0, :]
    local_inner = full_out.shape[0]
    local_heads = w_split.shape[1] - 2 * local_inner
    state_size = full_bc.shape[1] // 2
    taps_less = KC - 1
    seq_tokens = tokens[0]
    seq_cotan = cotangent[0]
    rows_here = seq_tokens.shape[0]
    split_row = vec_split[0]
    conv_x_w = split_row[: KC * local_inner].reshape(KC, local_inner)
    conv_end = KC * local_inner
    conv_x_b = split_row[conv_end : conv_end + local_inner]
    gate_gain = split_row[conv_end + local_inner : conv_end + 2 * local_inner]
    head_base = conv_end + 2 * local_inner
    step_bias = split_row[head_base : head_base + local_heads]
    rate_log = split_row[head_base + local_heads : head_base + 2 * local_heads]
    skip_gain = split_row[head_base + 2 * local_heads :]
    norm_gain = vec_rep[:D]
    conv_bc_w = vec_rep[D : D + KC * 2 * state_size].reshape(KC, 2 * state_size)
    conv_bc_b = vec_rep[D + KC * 2 * state_size :]
    conv_all_w = jnp.concatenate([conv_x_w, conv_bc_w], axis=1)
    conv_all_b = jnp.concatenate([conv_x_b, conv_bc_b])
    inv_rms = lax.rsqrt(jnp.mean(seq_tokens * seq_tokens, axis=1, keepdims=True) + norm_eps)
    normed = (seq_tokens * inv_rms * norm_gain[None, :]).astype(jnp.bfloat16)
    rim_tokens = shifted(seq_tokens[rows_here - taps_less :], "ctx", 1)
    rim_rms = lax.rsqrt(jnp.mean(rim_tokens * rim_tokens, axis=1, keepdims=True) + norm_eps)
    rim_normed = (rim_tokens * rim_rms * norm_gain[None, :]).astype(jnp.bfloat16)
    rim_normed = jnp.concatenate([rim_normed, jnp.zeros((16 - taps_less, D), jnp.bfloat16)], axis=0)
    proj_split = jnp.dot(normed, w_split, preferred_element_type=jnp.float32)
    proj_bc = jnp.dot(normed, full_bc, preferred_element_type=jnp.float32)
    proj_z = proj_split[:, :local_inner]
    proj_dt = proj_split[:, 2 * local_inner :]
    pre_conv = jnp.concatenate([proj_split[:, local_inner : 2 * local_inner], proj_bc], axis=1)
    rim_rows = jnp.concatenate(
        [
            jnp.dot(
                rim_normed,
                w_split[:, local_inner : 2 * local_inner],
                preferred_element_type=jnp.float32,
            ),
            jnp.dot(rim_normed, full_bc, preferred_element_type=jnp.float32),
        ],
        axis=1,
    )[:taps_less]
    padded = jnp.concatenate([rim_rows, pre_conv], axis=0)
    activated, conv_back = jax.vjp(conv_apply, padded, conv_all_w, conv_all_b)
    x_cols = activated[:, :local_inner]
    b_state = activated[:, local_inner : local_inner + state_size]
    c_state = activated[:, local_inner + state_size :]
    mixer_out, mixer_back = jax.vjp(
        local_mixer, x_cols, b_state, c_state, proj_dt, step_bias, rate_log, skip_gain
    )
    zero_mixed, local_state, decay_dev, cumulated = mixer_out
    decays, states = collect(decay_dev, local_state)
    start_state = entering(decays, states, "ctx", False)
    carried, carry_back = jax.vjp(carried_in, cumulated, c_state, start_state)
    mixed = (zero_mixed + carried).reshape(rows_here, local_inner)
    gate_act = jax.nn.silu(proj_z)
    gated = mixed * gate_act
    total_sq = lax.psum(jnp.sum(gated * gated, axis=1), "tp")
    gate_rms = lax.rsqrt(total_sq / E + norm_eps)[:, None]
    outnorm = (gated * gate_rms * gate_gain[None, :]).astype(jnp.bfloat16)
    out_part = jnp.dot(outnorm, full_out, preferred_element_type=jnp.float32)
    out_total = lax.psum(out_part, "tp")
    block_out = seq_tokens + out_total
    cotan_b = seq_cotan.astype(jnp.bfloat16)
    grad_norm_out = jnp.einsum("td,ed->te", cotan_b, full_out, preferred_element_type=jnp.float32)
    grad_w_out = jnp.einsum("td,te->de", cotan_b, outnorm, preferred_element_type=jnp.float32)
    inner_sum = lax.psum(jnp.sum(grad_norm_out * gate_gain[None, :] * gated, axis=1), "tp")
    grad_gate_gain = jnp.sum(grad_norm_out * gated * gate_rms, axis=0)
    grad_gated = (
        gate_rms * gate_gain[None, :] * grad_norm_out - gated * gate_rms**3 * inner_sum[:, None] / E
    )
    grad_mixed = (grad_gated * gate_act).reshape(rows_here, local_heads, local_inner // local_heads)
    sigmoid_z = jax.nn.sigmoid(proj_z)
    grad_z = grad_gated * mixed * sigmoid_z * (1.0 + proj_z * (1.0 - sigmoid_z))
    grad_cum, grad_c_carry, grad_start = carry_back(grad_mixed)
    grad_next = entering(decays, lax.all_gather(grad_start, "ctx"), "ctx", True)
    grad_decay = jnp.sum(grad_next * start_state, axis=(1, 2))
    grad_x, grad_b, grad_c, grad_dt, grad_step_bias, grad_rate_log, grad_skip = mixer_back(
        (grad_mixed, grad_next, grad_decay, grad_cum)
    )
    grad_c = grad_c + grad_c_carry
    grad_pad, grad_conv_w, grad_conv_b = conv_back(
        jnp.concatenate([grad_x, grad_b, grad_c], axis=1)
    )
    rim_grad = shift_back(grad_pad[:8])[:taps_less]
    grad_pre = grad_pad[taps_less:]
    grad_pre = jnp.concatenate(
        [grad_pre[: rows_here - taps_less], grad_pre[rows_here - taps_less :] + rim_grad], axis=0
    )
    grad_split = jnp.concatenate([grad_z, grad_pre[:, :local_inner], grad_dt], axis=1).astype(
        jnp.bfloat16
    )
    hidden_part = jnp.einsum("tc,dc->td", grad_split, w_split, preferred_element_type=jnp.float32)
    hidden_sum, grad_bc_pre, conv_bc_gw, conv_bc_gb = lax.psum(
        (
            hidden_part,
            grad_pre[:, local_inner:],
            grad_conv_w[:, local_inner:],
            grad_conv_b[local_inner:],
        ),
        "tp",
    )
    grad_bc = grad_bc_pre.astype(jnp.bfloat16)
    grad_hidden = hidden_sum + jnp.einsum(
        "tc,dc->td", grad_bc, full_bc, preferred_element_type=jnp.float32
    )
    grad_norm_gain = jnp.sum(grad_hidden * seq_tokens * inv_rms, axis=0)
    inner_in = jnp.mean(grad_hidden * norm_gain[None, :] * seq_tokens, axis=1, keepdims=True)
    grad_tokens = (
        seq_cotan + inv_rms * norm_gain[None, :] * grad_hidden - seq_tokens * inv_rms**3 * inner_in
    )
    tp_here = lax.axis_index("tp")
    half_bc = lax.dynamic_slice_in_dim(grad_bc, tp_here * state_size, state_size, axis=1)
    in_width = grad_split.shape[1]
    spare = jnp.zeros((rows_here, -in_width % lane), jnp.bfloat16)
    grad_cols = jnp.concatenate([grad_split, spare, half_bc], axis=1)
    grad_w_in = jnp.einsum("td,tc->dc", normed, grad_cols, preferred_element_type=jnp.float32)
    split_grad = jnp.concatenate(
        [
            grad_conv_w[:, :local_inner].reshape(-1),
            grad_conv_b[:local_inner],
            grad_gate_gain,
            grad_step_bias,
            grad_rate_log,
            grad_skip,
        ]
    )[None, :]
    rep_grad = jnp.concatenate([grad_norm_gain, conv_bc_gw.reshape(-1), conv_bc_gb])
    split_size, rep_size = split_grad.shape[1], rep_grad.shape[0]
    small_size = split_size + rep_size
    small = jnp.concatenate(
        [split_grad[0], rep_grad, jnp.zeros((-small_size % (8 * lane),), jnp.float32)]
    ).reshape(-1, lane)
    sum_a, sum_b, sum_pair, sum_small = reduce_grads(grad_w_in, grad_w_out, small)
    summed_in = sum_a[:, None, :in_width]
    mine_bc = sum_a[:, sum_a.shape[1] - state_size :]
    summed_bc = jnp.where(
        tp_here == 0,
        jnp.concatenate([mine_bc, sum_pair], axis=1),
        jnp.concatenate([sum_pair, mine_bc], axis=1),
    )
    summed_out = sum_b.T
    sum_small = sum_small.reshape(-1)
    split_sum = sum_small[:split_size][None, :]
    rep_sum = sum_small[split_size:small_size]
    new_in, new_mom_in = adam_step(mat_in, mom_in, summed_in)
    new_bc, new_mom_bc = adam_step(mat_bc, mom_bc, summed_bc)
    new_out, new_mom_out = adam_step(mat_out, mom_out, summed_out)
    new_split, new_mom_split = adam_step(vec_split, mom_split, split_sum)
    new_rep, new_mom_rep = adam_step(vec_rep, mom_rep, rep_sum)
    return (
        block_out[None],
        grad_tokens[None],
        new_in,
        new_bc,
        new_out,
        new_split,
        new_rep,
        new_mom_in,
        new_mom_bc,
        new_mom_out,
        new_mom_split,
        new_mom_rep,
    )


def solution(mesh):
    return jax.shard_map(
        shards,
        mesh=mesh,
        in_specs=(
            P("dp", "ctx", None),
            P("dp", "ctx", None),
            P("dp", "tp", None),
            P("dp", None),
            P("tp", "dp"),
            P("tp", None),
            P(),
            P(None, "dp", "tp", None),
            P(None, "dp", None),
            P(None, "tp", "dp"),
            P(None, "tp", None),
            P(),
        ),
        out_specs=(
            P("dp", "ctx", None),
            P("dp", "ctx", None),
            P("dp", "tp", None),
            P("dp", None),
            P("tp", "dp"),
            P("tp", None),
            P(),
            P(None, "dp", "tp", None),
            P(None, "dp", None),
            P(None, "tp", "dp"),
            P(None, "tp", None),
            P(),
        ),
        check_vma=False,
    )
```
